256 devices in a mesh: dp: 16 (over x, z_lo), width: 8 (over y, core), grid: 2 (over z_hi).
Axes of the slice: x: 4, y: 4, z: 8 (z_hi: 2, z_lo: 4; z = z_hi * 4 + z_lo), core: 2. Of those that a mesh axis runs over, the one named last changes fastest.
Arguments:
- train_acts: bfloat16 [12288, 16384], P(('dp', 'grid'), 'width'), may hold values from -6 to 6
- train_grads: bfloat16 [12288, 16384], P(('dp', 'grid'), 'width'), may hold values from -6 to 6
- query_acts: bfloat16 [512, 16384], P('dp', 'width'), may hold values from -6 to 6
- query_grads: bfloat16 [512, 16384], P('dp', 'width'), may hold values from -6 to 6
- act_inverse: bfloat16 [16384, 16384], P(('dp', 'grid'), 'width'), may hold values from -0.046875 to 0.046875
- grad_inverse: bfloat16 [16384, 16384], P(('dp', 'grid'), 'width'), may hold values from -0.046875 to 0.046875
- query_slot: int32 [16], replicated, may hold values from 0 to 15, each once
- resident: int32 [12288], P(('dp', 'grid')), may hold values 0 or 1
Outputs:
- scores: float32 [12288, 16], P(('dp', 'grid'), 'width')
The draws below stay inside these ranges and needn't reach their ends.
All inputs are finite; a program needn't handle non-finite values. No bound on the sum of `resident` on one device may be relied on, other than what follows from the above.
Results may differ from the reference program's by a relative error of at most 0.0041.
Values may be sent and summed in bfloat16 or wider, within the bound.
No kernel may reach another device: no remote copies, remote signals or barrier semaphores. Data moves between devices by JAX's collectives and lax.ppermute only.
A program may use at most 64 MiB of HBM per device.

```python
import math
import jax
import jax.numpy as jnp
from jax import lax

D = 16384
QDIM = 16384
QUERIES = 16
QTOK = 32
QROWS = 512
TRAIN = 12288


def with_ends(values, stream_key, smallest, high):
    longest = values.shape.index(max(values.shape))
    spots = []
    for shift in (0, 1):
        where = [jax.random.randint(jax.random.fold_in(stream_key, axis), (), 0, length) for axis, length in enumerate(values.shape)]
        where[longest] = (where[longest] + shift) % values.shape[longest]
        spots.append(tuple(where))
    return values.at[spots[0]].set(smallest).at[spots[1]].set(high)


def levels(stream_key, shape, cuts, least, high):
    def one(dim, shards_of):
        draws = jax.random.uniform(jax.random.fold_in(jax.random.fold_in(stream_key, 6), dim), (shards_of,), jnp.float32, least / len(cuts), high / len(cuts))
        return jnp.repeat(jnp.exp(draws), shape[dim] // shards_of).reshape((-1,) + (1,) * (len(shape) - dim - 1))

    loudness = one(*cuts[0])
    for cut in cuts[1:]:
        loudness = loudness * one(*cut)
    return loudness


def noise(rng, dims, spread, limit, split=(), kind=jnp.bfloat16):
    result = jax.random.normal(rng, dims, jnp.float32) * spread
    if len(split) > 0:
        result = levels(rng, dims, split, -0.22, 0.18) * result
    return jnp.clip(result, min=-limit, max=limit).astype(kind)


def setup_inputs(seed: int = 0) -> dict:
    splits = jax.random.split(jax.random.key(seed), 9)
    train_acts = noise(splits[0], (TRAIN, D), 1.0, 6.0, ((0, 32), (1, 8)))
    train_grads = noise(splits[1], (TRAIN, QDIM), 1.0, 6.0, ((0, 32), (1, 8)))
    query_acts = noise(splits[2], (QROWS, D), 1.0, 6.0, ((0, 16), (1, 8)))
    query_grads = noise(splits[3], (QROWS, QDIM), 1.0, 6.0, ((0, 16), (1, 8)))
    act_inverse = noise(splits[4], (D, D), D ** -0.5, 0.046875, ((0, 32), (1, 8)))
    grad_inverse = noise(splits[5], (QDIM, QDIM), QDIM ** -0.5, 0.046875, ((0, 32), (1, 8)))
    query_slot = jax.random.permutation(splits[6], QUERIES).astype(jnp.int32)
    resident = with_ends((jax.random.randint(splits[7], (TRAIN,), 0, 4) < 3).astype(jnp.int32), jax.random.fold_in(splits[7], 1), 0, 1)
    return {"train_acts": train_acts, "train_grads": train_grads, "query_acts": query_acts, "query_grads": query_grads, "act_inverse": act_inverse, "grad_inverse": grad_inverse, "query_slot": query_slot, "resident": resident}


def reference(train_acts, train_grads, query_acts, query_grads, act_inverse, grad_inverse, query_slot, resident):
    act_factor = jnp.dot(act_inverse, query_acts.T, preferred_element_type=jnp.float32).astype(jnp.bfloat16)
    grad_factor = jnp.dot(grad_inverse, query_grads.T, preferred_element_type=jnp.float32).astype(jnp.bfloat16)
    act_proj = jnp.dot(train_acts, act_factor, preferred_element_type=jnp.float32)
    grad_proj = jnp.dot(train_grads, grad_factor, preferred_element_type=jnp.float32)
    factor_scale = 1.0 / (D * math.sqrt(QTOK))
    influence = lax.optimization_barrier(jnp.sum((act_proj * grad_proj).reshape(act_proj.shape[0], QUERIES, QTOK), axis=2)) * factor_scale
    source = jnp.zeros((QUERIES,), jnp.int32).at[query_slot].set(jnp.arange(QUERIES, dtype=jnp.int32))
    return influence[:, source] * resident[:, None].astype(jnp.float32)
```

```python
import itertools
import math

import jax
import jax.numpy as jnp
from jax import lax
from jax.experimental import pallas as pl
from jax.experimental.pallas import tpu as pltpu
from jax.sharding import PartitionSpec as P

D = 16384
QUERIES = 16
QTOK = 32
AXES = ("dp", "width", "grid")
F32 = jnp.float32
BF16 = jnp.bfloat16


def device(x, y, z, c):
    x, y, z, c = x % 4, y % 4, z % 8, c % 2
    return ((4 * x + z % 4) * 8 + 2 * y + c) * 2 + z // 4


def move(target):
    return [
        (device(x, y, z, c), device(*target(x, y, z, c)))
        for x, y, z, c in itertools.product(range(4), range(4), range(8), range(2))
    ]


def along_x(value, step):
    return lax.ppermute(value, AXES, move(lambda x, y, z, c: (x + step, y, z, c)))


def along_y(value, step):
    return lax.ppermute(value, AXES, move(lambda x, y, z, c: (x, y + step, z, c)))


def along_z(value, step):
    return lax.ppermute(value, AXES, move(lambda x, y, z, c: (x, y, z + step, c)))


def other_core(value):
    return lax.ppermute(value, AXES, move(lambda x, y, z, c: (x, y, z, c + 1)))


def to_owner(value, step):
    def target(x, y, z, c):
        high, middle, low = z // 4, (z // 2) % 2, z % 2
        return (y + step, x, 4 * high + 2 * c + low, middle)

    return lax.ppermute(value, AXES, move(target))


def vmem():
    return pl.BlockSpec(memory_space=pltpu.VMEM)


def smem():
    return pl.BlockSpec(memory_space=pltpu.SMEM)


def anywhere():
    return pl.BlockSpec(memory_space=pl.ANY)


def chunk_row(slot_pair, y, c):
    core = lax.rem(slot_pair, 2)
    ahead = lax.rem(lax.div(slot_pair, 2) - y + 4, 4)
    return jnp.where(core == c, 256, 0) + ahead * 64


def nt_dot(a, b):
    return lax.dot_general(a, b, (((1,), (1,)), ((), ())), preferred_element_type=F32)


X_FROM = (0, -1, 1, 2)
Z_FROM = (0, -1, 1, 2)


def precondition_kernel(place, slots, *refs):
    a0, am, ap, ah, al, g0, gm, gp, gh, inv_a, inv_g, send, keep, rows, inv, sems = refs
    x, y, z, c = place[0], place[1], place[2], place[3]
    copies = [
        pltpu.make_async_copy(inv_a, inv.at[0], sems.at[0]),
        pltpu.make_async_copy(inv_g, inv.at[1], sems.at[1]),
    ]
    for copy in copies:
        copy.start()

    def put(array, source, query):
        slot = slots[query]
        row = chunk_row(lax.div(slot, 2), y, c) + 32 * lax.rem(slot, 2)
        target = rows.at[array, pl.ds(pl.multiple_of(row, 32), 32), :]
        copy = pltpu.make_async_copy(source, target, sems.at[2 + array])
        copy.start()
        return copy

    waits = ([], [])
    for i, dx in enumerate(X_FROM):
        column = lax.rem(x + dx + 4, 4) * 4
        for bundle, dz in ((a0, 0), (am, -1), (ap, 1)):
            waits[0].append(put(0, bundle.at[i], column + lax.rem(z + dz + 4, 4)))
        far = ah.at[i] if i < 2 else al.at[i - 2]
        waits[0].append(put(0, far, column + lax.rem(z + 2, 4)))
    for bundle, dx in ((g0, 0), (gm, -1), (gp, 1), (gh, 2)):
        column = lax.rem(x + dx + 4, 4) * 4
        for i, dz in enumerate(Z_FROM):
            waits[1].append(put(1, bundle.at[i], column + lax.rem(z + dz + 4, 4)))
    for array in range(2):
        copies[array].wait()
        for copy in waits[array]:
            copy.wait()
        for half, out in ((0, send), (1, keep)):
            for tile in range(2):
                out[array, :, 256 * tile : 256 * tile + 256] = nt_dot(
                    rows[array, 256 * half : 256 * half + 256, :],
                    inv[array, 256 * tile : 256 * tile + 256, :],
                )


def precondition(place, slots, acts, grads, inv_a, inv_g):
    half = jax.ShapeDtypeStruct((2, 256, 512), F32)
    return pl.pallas_call(
        precondition_kernel,
        out_shape=(half, half),
        in_specs=[smem(), smem()] + [anywhere()] * 11,
        out_specs=(vmem(), vmem()),
        scratch_shapes=[
            pltpu.VMEM((2, 512, 2048), BF16),
            pltpu.VMEM((2, 512, 2048), BF16),
            pltpu.SemaphoreType.DMA((4,)),
        ],
        name="precondition",
    )(place, slots, *acts, *grads, inv_a, inv_g)


def split_kernel(keep, got, *outs):
    for step, out in enumerate(outs):
        rows = slice(64 * step, 64 * step + 64)
        out[...] = keep[:, rows, :] + got[:, rows, :]


def split(keep, got):
    shape = jax.ShapeDtypeStruct((2, 64, keep.shape[-1]), F32)
    return pl.pallas_call(
        split_kernel,
        out_shape=(shape,) * 4,
        in_specs=[vmem()] * 2,
        out_specs=(vmem(),) * 4,
        name="split",
    )(keep, got)


def factor_kernel(p0, p1, p2, p3, acts, grads):
    for array, out in enumerate((acts, grads)):
        total = (p0[array] + p1[array]) + (p2[array] + p3[array])
        out[...] = total.astype(BF16)


def factor_sum(parts):
    shape = jax.ShapeDtypeStruct((64, 512), BF16)
    return pl.pallas_call(
        factor_kernel,
        out_shape=(shape, shape),
        in_specs=[vmem()] * 4,
        out_specs=(vmem(), vmem()),
        name="factor_sum",
    )(*parts)


RING = (0, -1, 1, -2, 2, -3, 3, 4)


def project_kernel(place, *refs):
    acts, grads, (tok_a, tok_g, send, keep, factor, tok, sems) = refs[:9], refs[9:13], refs[13:]
    x, y, z, c = place[0], place[1], place[2], place[3]
    ring = place[4]
    copies = [
        pltpu.make_async_copy(tok_a, tok.at[0], sems.at[0]),
        pltpu.make_async_copy(tok_g, tok.at[1], sems.at[1]),
    ]
    for copy in copies:
        copy.start()

    def put(array, source, dx, dz):
        px = lax.rem(x + dx + 4, 4)
        pz = lax.rem(ring + dz + 8, 8)
        row = chunk_row(2 * px + lax.rem(lax.div(pz, 2), 2), y, c)
        column = (2 * lax.rem(pz, 2) + lax.div(pz, 4)) * 512
        target = factor.at[
            array, pl.ds(pl.multiple_of(row, 64), 64), pl.ds(pl.multiple_of(column, 512), 512)
        ]
        copy = pltpu.make_async_copy(source, target, sems.at[2 + array])
        copy.start()
        return copy

    waits = ([], [])
    for bundle, dz in zip(acts[:7], RING):
        for i, dx in enumerate(X_FROM):
            waits[0].append(put(0, bundle.at[i], dx, dz))
    for i, dx in enumerate(X_FROM):
        source = acts[7].at[i] if i < 2 else acts[8].at[i - 2]
        waits[0].append(put(0, source, dx, 4))
    for bundle, dx in zip(grads, X_FROM):
        for i, dz in enumerate(RING):
            waits[1].append(put(1, bundle.at[i], dx, dz))
    for array in range(2):
        copies[array].wait()
        for copy in waits[array]:
            copy.wait()
        for half, out in ((0, send), (1, keep)):
            out[array] = nt_dot(factor[array, 256 * half : 256 * half + 256, :], tok[array])


def project(place, acts, grads, tok_a, tok_g):
    tokens = tok_a.shape[0]
    half = jax.ShapeDtypeStruct((2, 256, tokens), F32)
    return pl.pallas_call(
        project_kernel,
        out_shape=(half, half),
        in_specs=[smem()] + [anywhere()] * 15,
        out_specs=(vmem(), vmem()),
        scratch_shapes=[
            pltpu.VMEM((2, 512, 2048), BF16),
            pltpu.VMEM((2, tokens, 2048), BF16),
            pltpu.SemaphoreType.DMA((4,)),
        ],
        name="project",
    )(place, *acts, *grads, tok_a, tok_g)


def score_kernel(p0, p1, p2, p3, resident, out):
    acts = (p0[0] + p1[0]) + (p2[0] + p3[0])
    grads = (p0[1] + p1[1]) + (p2[1] + p3[1])
    product = acts * grads
    scale = 1.0 / (D * math.sqrt(QTOK))
    here = resident[...].astype(F32)
    for query in range(2):
        total = jnp.sum(product[QTOK * query : QTOK * query + QTOK], axis=0, keepdims=True)
        out[query : query + 1, :] = total * scale * here


def score(parts, resident):
    tokens = resident.shape[-1]
    return pl.pallas_call(
        score_kernel,
        out_shape=jax.ShapeDtypeStruct((2, tokens), F32),
        in_specs=[vmem()] * 5,
        out_specs=vmem(),
        name="score",
    )(*parts, resident)


def local(
    train_acts,
    train_grads,
    query_acts,
    query_grads,
    act_inverse,
    grad_inverse,
    query_slot,
    resident,
):
    dp, width, grid = (lax.axis_index(name) for name in AXES)
    place = jnp.stack([dp // 4, width // 2, dp % 4, width % 2, 4 * grid + dp % 4])

    ax = [query_acts] + [along_x(query_acts, step) for step in (1, -1, 2)]
    gz = [query_grads] + [along_z(query_grads, step) for step in (1, -1)]
    gz_far = [along_z(query_grads[:16], 2), along_z(query_grads[16:], -2)]
    gz.append(jnp.concatenate(gz_far, axis=0))
    a_bundle = jnp.stack(ax)
    g_bundle = jnp.stack(gz)
    acts = [a_bundle] + [along_z(a_bundle, step) for step in (1, -1)]
    acts += [along_z(a_bundle[:2], 2), along_z(a_bundle[2:], -2)]
    grads = [g_bundle] + [along_x(g_bundle, step) for step in (1, -1, 2)]

    send, keep = precondition(place, query_slot, acts, grads, act_inverse, grad_inverse)
    parts = split(keep, other_core(send))
    parts = [to_owner(part, step) for step, part in enumerate(parts)]
    fa, fg = factor_sum(parts)

    fa_bundle = jnp.stack([fa] + [along_x(fa, step) for step in (1, -1, 2)])

    def ring(own):
        got = [own]
        below, above = own, own
        for _ in range(3):
            below, above = along_z(below, 1), along_z(above, -1)
            got += [below, above]
        half = own.shape[0] // 2
        return got + [along_z(below[:half], 1), along_z(above[half:], -1)]

    acts = ring(fa_bundle)
    fg_ring = ring(fg)
    fg_bundle = jnp.stack(fg_ring[:7] + [jnp.concatenate(fg_ring[7:], axis=0)])
    grads = [fg_bundle] + [along_x(fg_bundle, step) for step in (1, -1, 2)]

    send, keep = project(place, acts, grads, train_acts, train_grads)
    parts = split(keep, other_core(send))
    parts = [parts[0]] + [along_y(parts[step], step) for step in (1, 2, 3)]
    return score(parts, resident.reshape(1, -1)).T


def solution(mesh):
    return jax.shard_map(
        local,
        mesh=mesh,
        in_specs=(
            P(("dp", "grid"), "width"),
            P(("dp", "grid"), "width"),
            P("dp", "width"),
            P("dp", "width"),
            P(("dp", "grid"), "width"),
            P(("dp", "grid"), "width"),
            P(),
            P(("dp", "grid")),
        ),
        out_specs=P(("dp", "grid"), "width"),
        check_vma=False,
    )
```

```python
import itertools
import math

import jax
import jax.numpy as jnp
from jax import lax
from jax.experimental import pallas as pl
from jax.experimental.pallas import tpu as pltpu
from jax.sharding import PartitionSpec as P

D = 16384
QUERIES = 16
QTOK = 32
AXES = ("dp", "width", "grid")
F32 = jnp.float32
BF16 = jnp.bfloat16


def device(x, y, z, c):
    x, y, z, c = x % 4, y % 4, z % 8, c % 2
    return ((4 * x + z % 4) * 8 + 2 * y + c) * 2 + z // 4


def move(target):
    return [
        (device(x, y, z, c), device(*target(x, y, z, c)))
        for x, y, z, c in itertools.product(range(4), range(4), range(8), range(2))
    ]


def along_x(value, step):
    return lax.ppermute(value, AXES, move(lambda x, y, z, c: (x + step, y, z, c)))


def along_y(value, step):
    return lax.ppermute(value, AXES, move(lambda x, y, z, c: (x, y + step, z, c)))


def along_z(value, step):
    return lax.ppermute(value, AXES, move(lambda x, y, z, c: (x, y, z + step, c)))


def other_core(value):
    return lax.ppermute(value, AXES, move(lambda x, y, z, c: (x, y, z, c + 1)))


def far_z(value):
    return lax.ppermute(value, AXES, move(lambda x, y, z, c: (x, y, z + 2 - 4 * c, c)))


def to_owner(value, step):
    def target(x, y, z, c):
        high, middle, low = z // 4, (z // 2) % 2, z % 2
        return (y, x, 4 * high + 2 * c + low + step, middle)

    return lax.ppermute(value, AXES, move(target))


def vmem():
    return pl.BlockSpec(memory_space=pltpu.VMEM)


def smem():
    return pl.BlockSpec(memory_space=pltpu.SMEM)


def anywhere():
    return pl.BlockSpec(memory_space=pl.ANY)


def chunk_row(slot_pair, y, c):
    core = lax.rem(slot_pair, 2)
    ahead = lax.rem(lax.div(slot_pair, 2) - y + 4, 4)
    return jnp.where(core == c, 256, 0) + ahead * 64


def nt_dot(a, b):
    return lax.dot_general(a, b, (((1,), (1,)), ((), ())), preferred_element_type=F32)


X_FROM = (0, -1, 1, 2)


def z_from(c):
    return (0, -1, 1, jnp.where(c == 0, -2, 2))


def precondition_kernel(place, slots, *refs):
    acts, grads, (inv_a, inv_g, send, keep, rows, inv, sems) = refs[:4], refs[4:8], refs[8:]
    x, y, z, c = place[0], place[1], place[2], place[3]
    copies = [
        pltpu.make_async_copy(inv_a, inv.at[0], sems.at[0]),
        pltpu.make_async_copy(inv_g, inv.at[1], sems.at[1]),
    ]
    for copy in copies:
        copy.start()

    def put(array, source, dx, dz):
        query = lax.rem(x + dx + 4, 4) * 4 + lax.rem(z + dz + 8, 4)
        slot = slots[query]
        row = chunk_row(lax.div(slot, 2), y, c) + 32 * lax.rem(slot, 2)
        target = rows.at[array, pl.ds(pl.multiple_of(row, 32), 32), :]
        copy = pltpu.make_async_copy(source, target, sems.at[2 + array])
        copy.start()
        return copy

    waits = ([], [])
    for bundle, dz in zip(acts, z_from(c)):
        for i, dx in enumerate(X_FROM):
            waits[0].append(put(0, bundle.at[i], dx, dz))
    for bundle, dx in zip(grads, X_FROM):
        for i, dz in enumerate(z_from(c)):
            waits[1].append(put(1, bundle.at[i], dx, dz))
    for array in range(2):
        copies[array].wait()
        for copy in waits[array]:
            copy.wait()
        for half, out in ((0, send), (1, keep)):

            def tile(t, _):
                at = pl.multiple_of(256 * t, 256)
                out[array, :, pl.ds(at, 256)] = nt_dot(
                    rows[array, 256 * half : 256 * half + 256, :], inv[array, pl.ds(at, 256), :]
                )
                return 0

            lax.fori_loop(0, 2, tile, 0)


def limit(mib):
    return pltpu.CompilerParams(vmem_limit_bytes=mib << 20)


def precondition(place, slots, acts, grads, inv_a, inv_g):
    half = jax.ShapeDtypeStruct((2, 256, 512), F32)
    return pl.pallas_call(
        precondition_kernel,
        out_shape=(half, half),
        in_specs=[smem(), smem()] + [anywhere()] * 10,
        out_specs=(vmem(), vmem()),
        scratch_shapes=[
            pltpu.VMEM((2, 512, 2048), BF16),
            pltpu.VMEM((2, 512, 2048), BF16),
            pltpu.SemaphoreType.DMA((4,)),
        ],
        compiler_params=limit(16),
        name="precondition",
    )(place, slots, *acts, *grads, inv_a, inv_g)


def split_kernel(keep, got, *outs):
    for step, out in enumerate(outs):
        rows = slice(64 * step, 64 * step + 64)
        out[...] = keep[:, rows, :] + got[:, rows, :]


def split(keep, got):
    shape = jax.ShapeDtypeStruct((2, 64, keep.shape[-1]), F32)
    return pl.pallas_call(
        split_kernel,
        out_shape=(shape,) * 4,
        in_specs=[vmem()] * 2,
        out_specs=(vmem(),) * 4,
        compiler_params=limit(6),
        name="split",
    )(keep, got)


def factor_kernel(p0, p1, p2, p3, out):
    out[...] = ((p0[...] + p1[...]) + (p2[...] + p3[...])).astype(BF16)


def factor_sum(parts):
    return pl.pallas_call(
        factor_kernel,
        out_shape=jax.ShapeDtypeStruct((2, 64, 512), BF16),
        in_specs=[vmem()] * 4,
        out_specs=vmem(),
        compiler_params=limit(4),
        name="factor_sum",
    )(*parts)


def project_kernel(place, *refs):
    acts, grads, (tok_a, tok_g, send, keep, factor, tok, sems) = refs[:4], refs[4:8], refs[8:]
    x, y, z, c = place[0], place[1], place[2], place[3]
    ring = place[4]
    copies = [
        pltpu.make_async_copy(tok_a, tok.at[0], sems.at[0]),
        pltpu.make_async_copy(tok_g, tok.at[1], sems.at[1]),
    ]
    for copy in copies:
        copy.start()

    def put(array, source, dx, dz):
        px = lax.rem(x + dx + 4, 4)
        pz = lax.rem(ring + dz + 8, 8)
        row = chunk_row(2 * px + lax.rem(lax.div(pz, 2), 2), y, c)
        column = (2 * lax.rem(pz, 2) + lax.div(pz, 4)) * 512
        target = factor.at[
            array, pl.ds(pl.multiple_of(row, 64), 64), pl.ds(pl.multiple_of(column, 512), 512)
        ]
        copy = pltpu.make_async_copy(source, target, sems.at[2 + array])
        copy.start()
        return copy

    waits = ([], [])
    for bundle, dz in zip(acts, z_from(c)):
        for i, dx in enumerate(X_FROM):
            for high in range(2):
                waits[0].append(put(0, bundle.at[i, high], dx, dz + 4 * high))
    for bundle, dx in zip(grads, X_FROM):
        for i, dz in enumerate(z_from(c)):
            for high in range(2):
                waits[1].append(put(1, bundle.at[i, high], dx, dz + 4 * high))
    for array in range(2):
        copies[array].wait()
        for copy in waits[array]:
            copy.wait()
        for half, out in ((0, send), (1, keep)):
            out[array] = nt_dot(factor[array, 256 * half : 256 * half + 256, :], tok[array])


def project(place, acts, grads, tok_a, tok_g):
    tokens = tok_a.shape[0]
    half = jax.ShapeDtypeStruct((2, 256, tokens), F32)
    return pl.pallas_call(
        project_kernel,
        out_shape=(half, half),
        in_specs=[smem()] + [anywhere()] * 10,
        out_specs=(vmem(), vmem()),
        scratch_shapes=[
            pltpu.VMEM((2, 512, 2048), BF16),
            pltpu.VMEM((2, tokens, 2048), BF16),
            pltpu.SemaphoreType.DMA((4,)),
        ],
        compiler_params=limit(16),
        name="project",
    )(place, *acts, *grads, tok_a, tok_g)


def score_kernel(p0, p1, p2, p3, resident, out):
    acts = (p0[0] + p1[0]) + (p2[0] + p3[0])
    grads = (p0[1] + p1[1]) + (p2[1] + p3[1])
    product = acts * grads
    scale = 1.0 / (D * math.sqrt(QTOK))
    here = resident[...].astype(F32)
    for query in range(2):
        total = jnp.sum(product[QTOK * query : QTOK * query + QTOK], axis=0, keepdims=True)
        out[query : query + 1, :] = total * scale * here


def score(parts, resident):
    tokens = resident.shape[-1]
    return pl.pallas_call(
        score_kernel,
        out_shape=jax.ShapeDtypeStruct((2, tokens), F32),
        in_specs=[vmem()] * 5,
        out_specs=vmem(),
        compiler_params=limit(6),
        name="score",
    )(*parts, resident)


def local(
    train_acts,
    train_grads,
    query_acts,
    query_grads,
    act_inverse,
    grad_inverse,
    query_slot,
    resident,
):
    dp, width, grid = (lax.axis_index(name) for name in AXES)
    place = jnp.stack([dp // 4, width // 2, dp % 4, width % 2, 4 * grid + dp % 4])

    def gather(acts, grads):
        ax = [acts] + [along_x(acts, step) for step in (1, -1, 2)]
        gz = [grads] + [along_z(grads, step) for step in (1, -1)] + [far_z(grads)]
        ax, gz = jnp.stack(ax), jnp.stack(gz)
        axz = [ax] + [along_z(ax, step) for step in (1, -1)] + [far_z(ax)]
        gzx = [gz] + [along_x(gz, step) for step in (1, -1, 2)]
        return axz, gzx

    acts, grads = gather(query_acts, query_grads)
    send, keep = precondition(place, query_slot, acts, grads, act_inverse, grad_inverse)
    parts = split(keep, other_core(send))
    factor = factor_sum([parts[0]] + [along_y(parts[step], step) for step in (1, 2, 3)])
    pair = [to_owner(factor, step) for step in (0, 4)]
    acts, grads = gather(*(jnp.stack([part[array] for part in pair]) for array in range(2)))
    send, keep = project(place, acts, grads, train_acts, train_grads)
    parts = split(keep, other_core(send))
    parts = [parts[0]] + [along_y(parts[step], step) for step in (1, 2, 3)]
    return score(parts, resident.reshape(1, -1)).T


def solution(mesh):
    return jax.shard_map(
        local,
        mesh=mesh,
        in_specs=(
            P(("dp", "grid"), "width"),
            P(("dp", "grid"), "width"),
            P("dp", "width"),
            P("dp", "width"),
            P(("dp", "grid"), "width"),
            P(("dp", "grid"), "width"),
            P(),
            P(("dp", "grid")),
        ),
        out_specs=P(("dp", "grid"), "width"),
        check_vma=False,
    )
```

```python
import itertools
import math

import jax
import jax.numpy as jnp
from jax import lax
from jax.experimental import pallas as pl
from jax.experimental.pallas import tpu as pltpu
from jax.sharding import PartitionSpec as P

D = 16384
QUERIES = 16
QTOK = 32
AXES = ("dp", "width", "grid")
F32 = jnp.float32
BF16 = jnp.bfloat16


def device(x, y, z, c):
    x, y, z, c = x % 4, y % 4, z % 8, c % 2
    return ((4 * x + z % 4) * 8 + 2 * y + c) * 2 + z // 4


def permute(value, target, sources=(0, 1)):
    pairs = [
        (device(x, y, z, c), device(*target(x, y, z, c)))
        for x, y, z, c in itertools.product(range(4), range(4), range(8), range(2))
        if c in sources
    ]
    return lax.ppermute(value, AXES, pairs)


def other_core(value, sources=(0, 1)):
    return permute(value, lambda x, y, z, c: (x, y, z, c + 1), sources)


def along_y(value, step):
    return permute(value, lambda x, y, z, c: (x, y + step, z, c))


def far(z):
    return -2 if z % 2 else 2


def spread(value, flip):
    def target(x_step, z_step):
        def to(x, y, z, c):
            if c == flip:
                return (x + x_step, y, z, c)
            return (x, y, z + (far(z) if z_step is None else z_step), c)

        return to

    return [permute(value, target(*steps)) for steps in ((2, None), (1, 1), (-1, -1))]


X_FROM = (0, 2, -1, 1)


def z_from(z):
    return (0, jnp.where(lax.rem(z, 2) == 0, -2, 2), -1, 1)


def offsets(c, z, first, second):
    zs = z_from(z)
    dx = jnp.where(c == 0, X_FROM[first], X_FROM[second])
    dz = jnp.where(c == 0, zs[second], zs[first])
    return dx, dz


def vmem():
    return pl.BlockSpec(memory_space=pltpu.VMEM)


def smem():
    return pl.BlockSpec(memory_space=pltpu.SMEM)


def anywhere():
    return pl.BlockSpec(memory_space=pl.ANY)


def limit(mib):
    return pltpu.CompilerParams(vmem_limit_bytes=mib << 20)


def nt_dot(a, b):
    return lax.dot_general(a, b, (((1,), (1,)), ((), ())), preferred_element_type=F32)


def both_halves(c, acts, grads, halves, sem):
    groups = []
    for core, sources in enumerate((acts, grads)):
        copies = [
            pltpu.make_async_copy(source, target, sem) for source, target in zip(sources, halves)
        ]
        groups.append(copies)

        @pl.when(c == core)
        def _(copies=copies):
            for copy in copies:
                copy.start()

    def wait():
        for core, copies in enumerate(groups):

            @pl.when(c == core)
            def _(copies=copies):
                for copy in copies:
                    copy.wait()

    return wait


def precondition_kernel(place, slots, *refs):
    bundles, (inv_a, inv_g, other_a, other_g), (outs, (rows, inv, sems)) = (
        refs[:4],
        refs[4:8],
        (refs[8:12], refs[12:]),
    )
    x, y, z, c = place[0], place[1], place[2], place[3]
    wait = both_halves(
        c, (inv_a, other_a), (inv_g, other_g), (inv.at[0], inv.at[1]), sems.at[0]
    )
    copies = []
    for second, bundle in enumerate(bundles):
        for first in range(4):
            dx, dz = offsets(c, z, first, second)
            query = lax.rem(x + dx + 4, 4) * 4 + lax.rem(z + dz + 8, 4)
            slot = slots[query]
            row = lax.rem(lax.div(slot, 4) - y + 4, 4) * 128 + 32 * lax.rem(slot, 4)
            target = rows.at[:, pl.ds(pl.multiple_of(row, 32), 32), :]
            copy = pltpu.make_async_copy(bundle.at[first], target, sems.at[1])
            copy.start()
            copies.append(copy)
    wait()
    for copy in copies:
        copy.wait()
    for step, out in enumerate(outs):
        at = slice(128 * step, 128 * step + 128)

        def tile(t, _):
            cols = pl.ds(pl.multiple_of(256 * t, 256), 256)
            out[:, cols] = nt_dot(rows[0, at, :], inv[0, cols, :]) + nt_dot(
                rows[1, at, :], inv[1, cols, :]
            )
            return 0

        lax.fori_loop(0, 2, tile, 0)


def precondition(place, slots, bundles, inverses):
    part = jax.ShapeDtypeStruct((128, 512), F32)
    return pl.pallas_call(
        precondition_kernel,
        out_shape=(part,) * 4,
        in_specs=[smem(), smem()] + [anywhere()] * 8,
        out_specs=(vmem(),) * 4,
        scratch_shapes=[
            pltpu.VMEM((2, 512, 2048), BF16),
            pltpu.VMEM((2, 512, 2048), BF16),
            pltpu.SemaphoreType.DMA((2,)),
        ],
        compiler_params=limit(16),
        name="precondition",
    )(place, slots, *bundles, *inverses)


def factor_kernel(p0, p1, p2, p3, out):
    out[...] = ((p0[...] + p1[...]) + (p2[...] + p3[...])).astype(BF16)


def factor_sum(parts):
    return pl.pallas_call(
        factor_kernel,
        out_shape=jax.ShapeDtypeStruct((128, 512), BF16),
        in_specs=[vmem()] * 4,
        out_specs=vmem(),
        compiler_params=limit(4),
        name="factor_sum",
    )(*parts)


def project_kernel(place, *refs):
    bundles, (tok_a, tok_g, other_a, other_g), (outs, (factor, tok, sems)) = (
        refs[:4],
        refs[4:8],
        (refs[8:12], refs[12:]),
    )
    x, y, z, c = place[0], place[1], place[2], place[3]
    wait = both_halves(
        c, (tok_a, other_a), (tok_g, other_g), (tok.at[c], tok.at[1 - c]), sems.at[0]
    )
    copies = []
    for second, bundle in enumerate(bundles):
        for first in range(4):
            dx, dz = offsets(c, z, first, second)
            px = lax.rem(x + dx + 4, 4)
            row = lax.rem(px - y + 4, 4) * 128
            for high in range(2):
                pz = lax.rem(z + dz + 4 * high + 8, 8)
                block = 2 * lax.rem(pz, 2) + lax.div(pz, 4)
                target = factor.at[
                    lax.rem(lax.div(pz, 2), 2),
                    pl.ds(pl.multiple_of(row, 128), 128),
                    pl.ds(pl.multiple_of(512 * block, 512), 512),
                ]
                copy = pltpu.make_async_copy(bundle.at[first, high], target, sems.at[1])
                copy.start()
                copies.append(copy)
    wait()
    for copy in copies:
        copy.wait()
    for step, out in enumerate(outs):
        at = slice(128 * step, 128 * step + 128)
        out[...] = nt_dot(factor[0, at, :], tok[0]) + nt_dot(factor[1, at, :], tok[1])


def project(place, bundles, tokens):
    count = tokens[0].shape[0]
    part = jax.ShapeDtypeStruct((128, count), F32)
    return pl.pallas_call(
        project_kernel,
        out_shape=(part,) * 4,
        in_specs=[smem()] + [anywhere()] * 8,
        out_specs=(vmem(),) * 4,
        scratch_shapes=[
            pltpu.VMEM((2, 512, 2048), BF16),
            pltpu.VMEM((2, count, 2048), BF16),
            pltpu.SemaphoreType.DMA((2,)),
        ],
        compiler_params=limit(16),
        name="project",
    )(place, *bundles, *tokens)


def sums_kernel(place, p0, p1, p2, p3, mine, give):
    c = place[3]
    total = (p0[...] + p1[...]) + (p2[...] + p3[...])
    low, high = total[:64], total[64:]
    mine[...] = jnp.where(c == 0, low, high)
    give[...] = jnp.where(c == 0, high, low)


def sums(place, parts):
    half = jax.ShapeDtypeStruct((64, parts[0].shape[1]), F32)
    return pl.pallas_call(
        sums_kernel,
        out_shape=(half, half),
        in_specs=[smem()] + [vmem()] * 4,
        out_specs=(vmem(), vmem()),
        compiler_params=limit(4),
        name="sums",
    )(place, *parts)


def score_kernel(mine, got, resident, out):
    product = mine[...] * got[...]
    scale = 1.0 / (D * math.sqrt(QTOK))
    here = resident[...].astype(F32)
    for query in range(2):
        total = jnp.sum(product[QTOK * query : QTOK * query + QTOK], axis=0, keepdims=True)
        out[query : query + 1, :] = total * scale * here


def score(mine, got, resident):
    return pl.pallas_call(
        score_kernel,
        out_shape=jax.ShapeDtypeStruct((2, resident.shape[-1]), F32),
        in_specs=[vmem()] * 3,
        out_specs=vmem(),
        compiler_params=limit(4),
        name="score",
    )(mine, got, resident)


def gather(own):
    bundle = jnp.stack([own] + spread(own, 0))
    return [bundle] + spread(bundle, 1)


def local(
    train_acts,
    train_grads,
    query_acts,
    query_grads,
    act_inverse,
    grad_inverse,
    query_slot,
    resident,
):
    dp, width, grid = (lax.axis_index(name) for name in AXES)
    core = width % 2
    place = jnp.stack([dp // 4, width // 2, 4 * grid + dp % 4, core])

    mine = jnp.where(core == 0, query_acts, query_grads)
    give = jnp.where(core == 0, query_grads, query_acts)
    bundles = gather(jnp.stack([mine, other_core(give)]))
    inverses = [act_inverse, grad_inverse]
    inverses += [other_core(act_inverse, (1,)), other_core(grad_inverse, (0,))]
    tokens = [train_acts, train_grads]
    tokens += [other_core(train_acts, (1,)), other_core(train_grads, (0,))]

    def sum_over_y(parts):
        return [parts[0]] + [along_y(parts[step], step) for step in (2, 1, 3)]

    factor = factor_sum(sum_over_y(precondition(place, query_slot, bundles, inverses)))
    pair = [
        permute(factor, lambda x, y, z, c, step=step: (y, x, z + step, c)) for step in (4, 0)
    ][::-1]
    parts = project(place, gather(jnp.stack(pair)), tokens)
    mine, give = sums(place, sum_over_y(parts))
    return score(mine, other_core(give), resident.reshape(1, -1)).T


def solution(mesh):
    return jax.shard_map(
        local,
        mesh=mesh,
        in_specs=(
            P(("dp", "grid"), "width"),
            P(("dp", "grid"), "width"),
            P("dp", "width"),
            P("dp", "width"),
            P(("dp", "grid"), "width"),
            P(("dp", "grid"), "width"),
            P(),
            P(("dp", "grid")),
        ),
        out_specs=P(("dp", "grid"), "width"),
        check_vma=False,
    )
```

```python
import itertools
import math

import jax
import jax.numpy as jnp
from jax import lax
from jax.experimental import pallas as pl
from jax.experimental.pallas import tpu as pltpu
from jax.sharding import PartitionSpec as P


D = 16384
QTOK = 32
AXES = ("dp", "width", "grid")
F32 = jnp.float32
BF16 = jnp.bfloat16


def device(x, y, z, c):
    x, y, z, c = x % 4, y % 4, z % 8, c % 2
    return ((4 * x + z % 4) * 8 + 2 * y + c) * 2 + z // 4


def move(target):
    return [
        (device(x, y, z, c), device(*target(x, y, z, c)))
        for x, y, z, c in itertools.product(range(4), range(4), range(8), range(2))
    ]


def along_x(value, step):
    return lax.ppermute(value, AXES, move(lambda x, y, z, c: (x + step, y, z, c)))


def along_y(value, step):
    return lax.ppermute(value, AXES, move(lambda x, y, z, c: (x, y + step, z, c)))


def along_z(value, step):
    return lax.ppermute(value, AXES, move(lambda x, y, z, c: (x, y, z + step, c)))


def other_core(value):
    return lax.ppermute(value, AXES, move(lambda x, y, z, c: (x, y, z, c + 1)))


def far_z(value):
    return lax.ppermute(value, AXES, move(lambda x, y, z, c: (x, y, z + 2 - 4 * c, c)))


def to_owner(value, step):
    def target(x, y, z, c):
        high, middle, low = z // 4, (z // 2) % 2, z % 2
        return (x + y, x, 4 * high + 2 * c + low + step, middle)

    return lax.ppermute(value, AXES, move(target))


def vmem():
    return pl.BlockSpec(memory_space=pltpu.VMEM)


def smem():
    return pl.BlockSpec(memory_space=pltpu.SMEM)


def anywhere():
    return pl.BlockSpec(memory_space=pl.ANY)


def chunk_row(slot_pair, y, c):
    core = lax.rem(slot_pair, 2)
    ahead = lax.rem(lax.div(slot_pair, 2) - y + 4, 4)
    return jnp.where(core == c, 256, 0) + ahead * 64


def nt_dot(a, b):
    return lax.dot_general(a, b, (((1,), (1,)), ((), ())), preferred_element_type=F32)


X_FROM = (0, 2, -1, 1)


def z_from(c):
    return (0, jnp.where(c == 0, -2, 2), -1, 1)


def precondition_kernel(place, slots, *refs):
    acts, grads, (inv_a, inv_g, send, rows, sems) = refs[:4], refs[4:8], refs[8:]
    x, y, z, c = place[0], place[1], place[2], place[3]

    def put(array, source, dx, dz):
        query = lax.rem(x + dx + 4, 4) * 4 + lax.rem(z + dz + 8, 4)
        slot = slots[query]
        row = chunk_row(lax.div(slot, 2), y, c) + 32 * lax.rem(slot, 2)
        target = rows.at[array, pl.ds(pl.multiple_of(row, 32), 32), :]
        copy = pltpu.make_async_copy(source, target, sems.at[array])
        copy.start()
        return copy

    waits = ([], [])
    for bundle, dz in zip(acts, z_from(c)):
        for i, dx in enumerate(X_FROM):
            waits[0].append(put(0, bundle.at[i], dx, dz))
    for bundle, dx in zip(grads, X_FROM):
        for i, dz in enumerate(z_from(c)):
            waits[1].append(put(1, bundle.at[i], dx, dz))
    for array, inv in enumerate((inv_a, inv_g)):
        for copy in waits[array]:
            copy.wait()
        tiles(send, rows, inv, array, 0)


def tiles(out, rows, inv, array, first):
    def tile(t, _):
        at = pl.multiple_of(256 * t, 256)
        out[array, :, pl.ds(at, 256)] = nt_dot(
            rows[array, first : first + 256, :], inv[pl.ds(at, 256), :]
        )
        return 0

    lax.fori_loop(0, inv.shape[0] // 256, tile, 0)


def keep_kernel(rows, inv_a, inv_g, keep):
    for array, inv in enumerate((inv_a, inv_g)):
        tiles(keep, rows, inv, array, 256)


def limit(mib):
    return pltpu.CompilerParams(vmem_limit_bytes=mib << 20)


def precondition(place, slots, acts, grads, inv_a, inv_g):
    return pl.pallas_call(
        precondition_kernel,
        out_shape=(
            jax.ShapeDtypeStruct((2, 256, 512), F32),
            jax.ShapeDtypeStruct((2, 512, 2048), BF16),
        ),
        in_specs=[smem(), smem()] + [anywhere()] * 8 + [vmem()] * 2,
        out_specs=(vmem(), vmem()),
        scratch_shapes=[pltpu.SemaphoreType.DMA((2,))],
        compiler_params=limit(16),
        name="precondition",
    )(place, slots, *acts, *grads, inv_a, inv_g)


def precondition_keep(rows, inv_a, inv_g):
    return pl.pallas_call(
        keep_kernel,
        out_shape=jax.ShapeDtypeStruct((2, 256, 512), F32),
        in_specs=[vmem()] * 3,
        out_specs=vmem(),
        compiler_params=limit(16),
        cost_estimate=pl.CostEstimate(flops=2**30, bytes_accessed=2**20, transcendentals=0),
        name="precondition_keep",
    )(rows, inv_a, inv_g)


def split_kernel(keep, got, *outs):
    for step, out in enumerate(outs):
        rows = slice(64 * step, 64 * step + 64)
        out[...] = keep[:, rows, :] + got[:, rows, :]


def split(keep, got):
    shape = jax.ShapeDtypeStruct((2, 64, keep.shape[-1]), F32)
    return pl.pallas_call(
        split_kernel,
        out_shape=(shape,) * 4,
        in_specs=[vmem()] * 2,
        out_specs=(vmem(),) * 4,
        compiler_params=limit(6),
        name="split",
    )(keep, got)


def factor_kernel(p0, p1, p2, p3, out):
    out[...] = ((p0[...] + p1[...]) + (p2[...] + p3[...])).astype(BF16)


def factor_sum(parts):
    return pl.pallas_call(
        factor_kernel,
        out_shape=jax.ShapeDtypeStruct((2, 64, 512), BF16),
        in_specs=[vmem()] * 4,
        out_specs=vmem(),
        compiler_params=limit(4),
        name="factor_sum",
    )(*parts)


def project_kernel(place, *refs):
    acts, grads, (tok_a, tok_g, send, factor, sems) = refs[:4], refs[4:8], refs[8:]
    x, y, c = place[0], place[1], place[3]
    ring = place[4]

    def put(array, source, dx, dz):
        px = lax.rem(x + dx - y + 8, 4)
        pz = lax.rem(ring + dz + 8, 8)
        row = chunk_row(2 * px + lax.rem(lax.div(pz, 2), 2), y, c)
        column = (2 * lax.rem(pz, 2) + lax.div(pz, 4)) * 512
        target = factor.at[
            array, pl.ds(pl.multiple_of(row, 64), 64), pl.ds(pl.multiple_of(column, 512), 512)
        ]
        copy = pltpu.make_async_copy(source, target, sems.at[array])
        copy.start()
        return copy

    waits = ([], [])
    for bundle, dz in zip(acts, z_from(c)):
        for i, dx in enumerate(X_FROM):
            for high in range(2):
                waits[0].append(put(0, bundle.at[i, high], dx, dz + 4 * high))
    for bundle, dx in zip(grads, X_FROM):
        for i, dz in enumerate(z_from(c)):
            for high in range(2):
                waits[1].append(put(1, bundle.at[i, high], dx, dz + 4 * high))
    for array, tok in enumerate((tok_a, tok_g)):
        for copy in waits[array]:
            copy.wait()
        send[array] = nt_dot(factor[array, :256, :], tok[...])


def project_keep_kernel(factor, tok_a, tok_g, keep):
    for array, tok in enumerate((tok_a, tok_g)):
        keep[array] = nt_dot(factor[array, 256:, :], tok[...])


def project(place, acts, grads, tok_a, tok_g):
    return pl.pallas_call(
        project_kernel,
        out_shape=(
            jax.ShapeDtypeStruct((2, 256, tok_a.shape[0]), F32),
            jax.ShapeDtypeStruct((2, 512, 2048), BF16),
        ),
        in_specs=[smem()] + [anywhere()] * 8 + [vmem()] * 2,
        out_specs=(vmem(), vmem()),
        scratch_shapes=[pltpu.SemaphoreType.DMA((2,))],
        compiler_params=limit(16),
        name="project",
    )(place, *acts, *grads, tok_a, tok_g)


def project_keep(factor, tok_a, tok_g):
    return pl.pallas_call(
        project_keep_kernel,
        out_shape=jax.ShapeDtypeStruct((2, 256, tok_a.shape[0]), F32),
        in_specs=[vmem()] * 3,
        out_specs=vmem(),
        compiler_params=limit(16),
        cost_estimate=pl.CostEstimate(flops=2**30, bytes_accessed=2**20, transcendentals=0),
        name="project_keep",
    )(factor, tok_a, tok_g)


def score_kernel(p0, p1, p2, p3, resident, out):
    acts = (p0[0] + p1[0]) + (p2[0] + p3[0])
    grads = (p0[1] + p1[1]) + (p2[1] + p3[1])
    product = acts * grads
    scale = 1.0 / (D * math.sqrt(QTOK))
    here = resident[...].astype(F32)
    for query in range(2):
        total = jnp.sum(product[QTOK * query : QTOK * query + QTOK], axis=0, keepdims=True)
        out[query : query + 1, :] = total * scale * here


def score(parts, resident):
    tokens = resident.shape[-1]
    return pl.pallas_call(
        score_kernel,
        out_shape=jax.ShapeDtypeStruct((2, tokens), F32),
        in_specs=[vmem()] * 5,
        out_specs=vmem(),
        compiler_params=limit(6),
        name="score",
    )(*parts, resident)


def local(
    train_acts,
    train_grads,
    query_acts,
    query_grads,
    act_inverse,
    grad_inverse,
    query_slot,
    resident,
):
    dp, width, grid = (lax.axis_index(name) for name in AXES)
    place = jnp.stack([dp // 4, width // 2, dp % 4, width % 2, 4 * grid + dp % 4])

    def x_others(value):
        out = []
        for step in (2, 1, -1):
            out.append(along_x(value, step))
        return out

    def z_others(value):
        out = [far_z(value)]
        for step in (1, -1):
            out.append(along_z(value, step))
        return out

    def gather(acts, grads):
        gz = jnp.stack([grads] + z_others(grads))
        ax = jnp.stack([acts] + x_others(acts))
        gzx = [gz] + x_others(gz)
        axz = [ax] + z_others(ax)
        return axz, gzx

    acts, grads = gather(query_acts, query_grads)
    send, rows = precondition(place, query_slot, acts, grads, act_inverse, grad_inverse)
    got = other_core(send)
    parts = split(precondition_keep(rows, act_inverse, grad_inverse), got)
    moved = [parts[0]]
    for step in (2, 1, 3):
        moved.append(along_y(parts[step], step))
    factor = factor_sum(moved)
    far = to_owner(factor, 4)
    near = to_owner(factor, 0)
    acts, grads = gather(*(jnp.stack([near[array], far[array]]) for array in range(2)))
    send, rows = project(place, acts, grads, train_acts, train_grads)
    got = other_core(send)
    parts = split(project_keep(rows, train_acts, train_grads), got)
    moved = [parts[0]]
    for step in (2, 1, 3):
        moved.append(along_y(parts[step], step))
    return score(moved, resident.reshape(1, -1)).T


def solution(mesh):
    return jax.shard_map(
        local,
        mesh=mesh,
        in_specs=(
            P(("dp", "grid"), "width"),
            P(("dp", "grid"), "width"),
            P("dp", "width"),
            P("dp", "width"),
            P(("dp", "grid"), "width"),
            P(("dp", "grid"), "width"),
            P(),
            P(("dp", "grid")),
        ),
        out_specs=P(("dp", "grid"), "width"),
        check_vma=False,
    )
```

```python
import functools
import itertools
import math

import jax
import jax.numpy as jnp
from jax import lax
from jax.experimental import pallas as pl
from jax.experimental.pallas import tpu as pltpu
from jax.sharding import PartitionSpec as P


D = 16384
QTOK = 32
AXES = ("dp", "width", "grid")
F32 = jnp.float32
BF16 = jnp.bfloat16


def device(x, y, z, c):
    x, y, z, c = x % 4, y % 4, z % 8, c % 2
    return ((4 * x + z % 4) * 8 + 2 * y + c) * 2 + z // 4


def move(target):
    return [
        (device(x, y, z, c), device(*target(x, y, z, c)))
        for x, y, z, c in itertools.product(range(4), range(4), range(8), range(2))
    ]


def along_x(value, step):
    return lax.ppermute(value, AXES, move(lambda x, y, z, c: (x + step, y, z, c)))


def along_y(value, step):
    return lax.ppermute(value, AXES, move(lambda x, y, z, c: (x, y + step, z, c)))


def along_z(value, step):
    return lax.ppermute(value, AXES, move(lambda x, y, z, c: (x, y, z + step, c)))


def other_core(value):
    return lax.ppermute(value, AXES, move(lambda x, y, z, c: (x, y, z, c + 1)))


def far_z(value):
    return lax.ppermute(value, AXES, move(lambda x, y, z, c: (x, y, z + 2 - 4 * c, c)))


def to_owner(value, step):
    def target(x, y, z, c):
        high, middle, low = z // 4, (z // 2) % 2, z % 2
        return (x + y, x, 4 * high + 2 * c + low + step, middle)

    return lax.ppermute(value, AXES, move(target))


def vmem():
    return pl.BlockSpec(memory_space=pltpu.VMEM)


def smem():
    return pl.BlockSpec(memory_space=pltpu.SMEM)


def anywhere():
    return pl.BlockSpec(memory_space=pl.ANY)


def chunk_row(slot_pair, y, c):
    core = lax.rem(slot_pair, 2)
    ahead = lax.rem(lax.div(slot_pair, 2) - y + 4, 4)
    return jnp.where(core == c, 256, 0) + ahead * 64


def nt_dot(a, b):
    return lax.dot_general(a, b, (((1,), (1,)), ((), ())), preferred_element_type=F32)


X_FROM = (0, 2, -1, 1)


def z_from(c):
    return (0, jnp.where(c == 0, -2, 2), -1, 1)


def tiles(out, rows, inv, first):
    def tile(t, _):
        at = pl.multiple_of(256 * t, 256)
        out[:, pl.ds(at, 256)] = nt_dot(rows[first : first + 256, :], inv[pl.ds(at, 256), :])
        return 0

    lax.fori_loop(0, inv.shape[0] // 256, tile, 0)


def piece_offsets(z_first, c):
    for second in range(4):
        for first in range(4):
            if z_first:
                yield second, first, X_FROM[second], z_from(c)[first]
            else:
                yield second, first, X_FROM[first], z_from(c)[second]


def precondition_kernel(z_first, place, slots, *refs):
    bundles, (inv, send, rows, sem) = refs[:4], refs[4:]
    x, y, z, c = place[0], place[1], place[2], place[3]
    copies = []
    for second, first, dx, dz in piece_offsets(z_first, c):
        query = lax.rem(x + dx + 4, 4) * 4 + lax.rem(z + dz + 8, 4)
        slot = slots[query]
        row = chunk_row(lax.div(slot, 2), y, c) + 32 * lax.rem(slot, 2)
        target = rows.at[pl.ds(pl.multiple_of(row, 32), 32), :]
        copy = pltpu.make_async_copy(bundles[second].at[first], target, sem)
        copy.start()
        copies.append(copy)
    for copy in copies:
        copy.wait()
    tiles(send, rows, inv, 0)


def keep_kernel(rows, right, keep):
    tiles(keep, rows, right, 256)


def estimate():
    return pl.CostEstimate(flops=2**29, bytes_accessed=2**20, transcendentals=0)


def precondition(place, slots, bundles, inv, z_first):
    return pl.pallas_call(
        functools.partial(precondition_kernel, z_first),
        out_shape=(
            jax.ShapeDtypeStruct((256, 512), F32),
            jax.ShapeDtypeStruct((512, 2048), BF16),
        ),
        in_specs=[smem(), smem()] + [anywhere()] * 4 + [vmem()],
        out_specs=(vmem(),) * 2,
        scratch_shapes=[pltpu.SemaphoreType.DMA(())],
        compiler_params=limit(8),
        cost_estimate=estimate(),
        name="precondition",
    )(place, slots, *bundles, inv)


def kept(rows, right):
    return pl.pallas_call(
        keep_kernel if right.shape[0] % 256 == 0 else project_keep_kernel,
        out_shape=jax.ShapeDtypeStruct((256, right.shape[0]), F32),
        in_specs=[vmem()] * 2,
        out_specs=vmem(),
        compiler_params=limit(8),
        cost_estimate=estimate(),
    )(rows, right)


def stack_kernel(*refs):
    sources, (out, sems) = refs[:-2], refs[-2:]
    copies = [
        pltpu.make_async_copy(source, out.at[i], sems.at[i]) for i, source in enumerate(sources)
    ]
    for copy in copies:
        copy.start()
    for copy in copies:
        copy.wait()


def stack(*arrays):
    count = len(arrays)
    return pl.pallas_call(
        stack_kernel,
        out_shape=jax.ShapeDtypeStruct((count,) + arrays[0].shape, arrays[0].dtype),
        in_specs=[anywhere()] * count,
        out_specs=vmem(),
        scratch_shapes=[pltpu.SemaphoreType.DMA((count,))],
        compiler_params=limit(2),
        name="stack",
    )(*arrays)


def limit(mib):
    return pltpu.CompilerParams(vmem_limit_bytes=mib << 20)


def split_kernel(keep_a, keep_g, got_a, got_g, *outs):
    for step, out in enumerate(outs):
        rows = slice(64 * step, 64 * step + 64)
        out[0] = keep_a[rows, :] + got_a[rows, :]
        out[1] = keep_g[rows, :] + got_g[rows, :]


def split(keep, got):
    shape = jax.ShapeDtypeStruct((2, 64, keep[0].shape[-1]), F32)
    return pl.pallas_call(
        split_kernel,
        out_shape=(shape,) * 4,
        in_specs=[vmem()] * 4,
        out_specs=(vmem(),) * 4,
        compiler_params=limit(6),
        name="split",
    )(*keep, *got)


def factor_kernel(p0, p1, p2, p3, out):
    out[...] = ((p0[...] + p1[...]) + (p2[...] + p3[...])).astype(BF16)


def factor_sum(parts):
    return pl.pallas_call(
        factor_kernel,
        out_shape=jax.ShapeDtypeStruct((2, 64, 512), BF16),
        in_specs=[vmem()] * 4,
        out_specs=vmem(),
        compiler_params=limit(4),
        name="factor_sum",
    )(*parts)


def project_kernel(z_first, place, *refs):
    bundles, (tok, send, factor, sem) = refs[:4], refs[4:]
    x, y, c = place[0], place[1], place[3]
    ring = place[4]
    copies = []
    for second, first, dx, dz in piece_offsets(z_first, c):
        for high in range(2):
            px = lax.rem(x + dx - y + 8, 4)
            pz = lax.rem(ring + dz + 4 * high + 8, 8)
            row = chunk_row(2 * px + lax.rem(lax.div(pz, 2), 2), y, c)
            column = (2 * lax.rem(pz, 2) + lax.div(pz, 4)) * 512
            target = factor.at[
                pl.ds(pl.multiple_of(row, 64), 64), pl.ds(pl.multiple_of(column, 512), 512)
            ]
            copy = pltpu.make_async_copy(bundles[second].at[first, high], target, sem)
            copy.start()
            copies.append(copy)
    for copy in copies:
        copy.wait()
    send[...] = nt_dot(factor[:256, :], tok[...])


def project_keep_kernel(factor, tok, keep):
    keep[...] = nt_dot(factor[256:, :], tok[...])


def project(place, bundles, tok, z_first):
    return pl.pallas_call(
        functools.partial(project_kernel, z_first),
        out_shape=(
            jax.ShapeDtypeStruct((256, tok.shape[0]), F32),
            jax.ShapeDtypeStruct((512, 2048), BF16),
        ),
        in_specs=[smem()] + [anywhere()] * 4 + [vmem()],
        out_specs=(vmem(),) * 2,
        scratch_shapes=[pltpu.SemaphoreType.DMA(())],
        compiler_params=limit(8),
        cost_estimate=estimate(),
        name="project",
    )(place, *bundles, tok)


def score_kernel(p0, p1, p2, p3, resident, out):
    acts = (p0[0] + p1[0]) + (p2[0] + p3[0])
    grads = (p0[1] + p1[1]) + (p2[1] + p3[1])
    product = acts * grads
    scale = 1.0 / (D * math.sqrt(QTOK))
    here = resident[...].astype(F32)
    for query in range(2):
        total = jnp.sum(product[QTOK * query : QTOK * query + QTOK], axis=0, keepdims=True)
        out[query : query + 1, :] = total * scale * here


def score(parts, resident):
    tokens = resident.shape[-1]
    return pl.pallas_call(
        score_kernel,
        out_shape=jax.ShapeDtypeStruct((2, tokens), F32),
        in_specs=[vmem()] * 5,
        out_specs=vmem(),
        compiler_params=limit(6),
        name="score",
    )(*parts, resident)


def local(
    train_acts,
    train_grads,
    query_acts,
    query_grads,
    act_inverse,
    grad_inverse,
    query_slot,
    resident,
):
    dp, width, grid = (lax.axis_index(name) for name in AXES)
    place = jnp.stack([dp // 4, width // 2, dp % 4, width % 2, 4 * grid + dp % 4])
    place, query_slot, query_acts = lax.optimization_barrier((place, query_slot, query_acts))

    def x_others(value):
        out = []
        for step in (2, 1, -1):
            out.append(along_x(value, step))
        return out

    def z_others(value):
        out = [far_z(value)]
        for step in (1, -1):
            out.append(along_z(value, step))
        return out

    def gather(acts, grads):
        ax, gz = x_others(acts), z_others(grads)
        ax, gz = stack(acts, *ax), stack(grads, *gz)
        gzx = [gz] + x_others(gz)
        axz = [ax] + z_others(ax)
        return axz, gzx

    bundles = gather(query_acts, query_grads)
    halves = []
    for array, inv in enumerate((act_inverse, grad_inverse)):
        send, rows = precondition(place, query_slot, bundles[array], inv, array == 1)
        got = other_core(send)
        halves.append((kept(rows, inv), got))
    parts = split(*zip(*halves))
    moved = [parts[0]]
    for step in (2, 1, 3):
        moved.append(along_y(parts[step], step))
    factor = factor_sum(moved)
    owner_4 = to_owner(factor, 4)
    owner_0 = to_owner(factor, 0)
    bundles = gather(*(jnp.stack([owner_0[array], owner_4[array]]) for array in range(2)))
    halves = []
    for array, tok in enumerate((train_acts, train_grads)):
        send, rows = project(place, bundles[array], tok, array == 1)
        got = other_core(send)
        halves.append((kept(rows, tok), got))
    parts = split(*zip(*halves))
    moved = [parts[0]]
    for step in (2, 1, 3):
        moved.append(along_y(parts[step], step))
    return score(moved, resident.reshape(1, -1)).T


def solution(mesh):
    return jax.shard_map(
        local,
        mesh=mesh,
        in_specs=(
            P(("dp", "grid"), "width"),
            P(("dp", "grid"), "width"),
            P("dp", "width"),
            P("dp", "width"),
            P(("dp", "grid"), "width"),
            P(("dp", "grid"), "width"),
            P(),
            P(("dp", "grid")),
        ),
        out_specs=P(("dp", "grid"), "width"),
        check_vma=False,
    )
```

```python
import functools
import itertools
import math

import jax
import jax.numpy as jnp
from jax import lax
from jax.experimental import pallas as pl
from jax.experimental.pallas import tpu as pltpu
from jax.sharding import PartitionSpec as P


D = 16384
QTOK = 32
AXES = ("dp", "width", "grid")
F32 = jnp.float32
BF16 = jnp.bfloat16


def device(x, y, z, c):
    x, y, z, c = x % 4, y % 4, z % 8, c % 2
    return ((4 * x + z % 4) * 8 + 2 * y + c) * 2 + z // 4


def move(target):
    return [
        (device(x, y, z, c), device(*target(x, y, z, c)))
        for x, y, z, c in itertools.product(range(4), range(4), range(8), range(2))
    ]


def along_x(value, step):
    return lax.ppermute(value, AXES, move(lambda x, y, z, c: (x + step, y, z, c)))


def along_y(value, step):
    return lax.ppermute(value, AXES, move(lambda x, y, z, c: (x, y + step, z, c)))


def along_z(value, step):
    return lax.ppermute(value, AXES, move(lambda x, y, z, c: (x, y, z + step, c)))


def other_core(value):
    return lax.ppermute(value, AXES, move(lambda x, y, z, c: (x, y, z, c + 1)))


def far_z(value):
    return lax.ppermute(value, AXES, move(lambda x, y, z, c: (x, y, z + 2 - 4 * c, c)))


def to_owner(value, step):
    def target(x, y, z, c):
        high, middle, low = z // 4, (z // 2) % 2, z % 2
        return (x + y, x, 4 * high + 2 * c + low + step, middle)

    return lax.ppermute(value, AXES, move(target))


def vmem():
    return pl.BlockSpec(memory_space=pltpu.VMEM)


def smem():
    return pl.BlockSpec(memory_space=pltpu.SMEM)


def chunk_row(slot_pair, y, c):
    core = lax.rem(slot_pair, 2)
    ahead = lax.rem(lax.div(slot_pair, 2) - y + 4, 4)
    return jnp.where(core == c, 256, 0) + ahead * 64


def nt_dot(a, b):
    return lax.dot_general(a, b, (((1,), (1,)), ((), ())), preferred_element_type=F32)


X_FROM = (0, 2, -1, 1)


def z_from(c):
    return (0, jnp.where(c == 0, -2, 2), -1, 1)


def tiles(out, rows, inv, first):
    def tile(t, _):
        at = pl.multiple_of(256 * t, 256)
        out[:, pl.ds(at, 256)] = nt_dot(rows[first : first + 256, :], inv[pl.ds(at, 256), :])
        return 0

    lax.fori_loop(0, inv.shape[0] // 256, tile, 0)


def piece_offsets(z_first, c):
    for second in range(4):
        for first in range(4):
            if z_first:
                yield second, first, X_FROM[second], z_from(c)[first]
            else:
                yield second, first, X_FROM[first], z_from(c)[second]


def precondition_kernel(z_first, place, slots, *refs):
    bundles, (inv, send, rows) = refs[:4], refs[4:]
    x, y, z, c = place[0], place[1], place[2], place[3]
    for second, first, dx, dz in piece_offsets(z_first, c):
        query = lax.rem(x + dx + 4, 4) * 4 + lax.rem(z + dz + 8, 4)
        slot = slots[query]
        row = chunk_row(lax.div(slot, 2), y, c) + 32 * lax.rem(slot, 2)
        rows[pl.ds(pl.multiple_of(row, 32), 32), :] = bundles[second][first]
    tiles(send, rows, inv, 0)


def keep_kernel(rows, right, keep):
    tiles(keep, rows, right, 256)


def estimate():
    return pl.CostEstimate(flops=2**29, bytes_accessed=2**20, transcendentals=0)


def precondition(place, slots, bundles, inv, z_first):
    return pl.pallas_call(
        functools.partial(precondition_kernel, z_first),
        out_shape=(
            jax.ShapeDtypeStruct((256, 512), F32),
            jax.ShapeDtypeStruct((512, 2048), BF16),
        ),
        in_specs=[smem(), smem()] + [vmem()] * 5,
        out_specs=(vmem(),) * 2,
        compiler_params=limit(8),
        cost_estimate=estimate(),
        name="precondition",
    )(place, slots, *bundles, inv)


def kept(rows, right):
    return pl.pallas_call(
        keep_kernel if right.shape[0] % 256 == 0 else project_keep_kernel,
        out_shape=jax.ShapeDtypeStruct((256, right.shape[0]), F32),
        in_specs=[vmem()] * 2,
        out_specs=vmem(),
        compiler_params=limit(8),
        cost_estimate=estimate(),
    )(rows, right)


def limit(mib):
    return pltpu.CompilerParams(vmem_limit_bytes=mib << 20)


BITS = 14


def code(values):
    largest = jnp.max(jnp.abs(values), axis=(0, 1), keepdims=True)
    power = jnp.ceil(jnp.log2(jnp.maximum(largest, 1e-30)))
    whole = jnp.floor(values * jnp.exp2(BITS - power) + 0.5)
    return whole.astype(jnp.int32), jnp.broadcast_to(power, (8, values.shape[1])).astype(jnp.int32)


def coded(block, array):
    power = block[128 + 8 * array : 136 + 8 * array, :].astype(jnp.int32).astype(F32)[:1]
    whole = block[64 * array : 64 * array + 64, :].astype(jnp.int32).astype(F32)
    return whole * jnp.exp2(power - BITS)


def split_kernel(keep_a, keep_g, got_a, got_g, own, *outs):
    for step in range(4):
        rows = slice(64 * step, 64 * step + 64)
        sums = keep_a[rows, :] + got_a[rows, :], keep_g[rows, :] + got_g[rows, :]
        if step == 0:
            own[0], own[1] = sums
        else:
            (acts, power_a), (grads, power_g) = map(code, sums)
            block = jnp.concatenate([acts, grads, power_a, power_g], axis=0)
            outs[step - 1][...] = block.astype(jnp.int16)


def split(keep, got):
    width = keep[0].shape[-1]
    return pl.pallas_call(
        split_kernel,
        out_shape=(jax.ShapeDtypeStruct((2, 64, width), F32),)
        + (jax.ShapeDtypeStruct((144, width), jnp.int16),) * 3,
        in_specs=[vmem()] * 4,
        out_specs=(vmem(),) * 4,
        compiler_params=limit(6),
        name="split",
    )(*keep, *got)


def total(p0, p1, p2, p3, array):
    return (p0[array] + coded(p1, array)) + (coded(p2, array) + coded(p3, array))


def factor_kernel(p0, p1, p2, p3, out):
    for array in range(2):
        out[array] = total(p0, p1, p2, p3, array).astype(BF16)


def factor_sum(parts):
    return pl.pallas_call(
        factor_kernel,
        out_shape=jax.ShapeDtypeStruct((2, 64, 512), BF16),
        in_specs=[vmem()] * 4,
        out_specs=vmem(),
        compiler_params=limit(4),
        name="factor_sum",
    )(*parts)


def project_kernel(z_first, place, *refs):
    bundles, (tok, send, factor) = refs[:4], refs[4:]
    x, y, c = place[0], place[1], place[3]
    ring = place[4]
    for second, first, dx, dz in piece_offsets(z_first, c):
        for high in range(2):
            px = lax.rem(x + dx - y + 8, 4)
            pz = lax.rem(ring + dz + 4 * high + 8, 8)
            row = chunk_row(2 * px + lax.rem(lax.div(pz, 2), 2), y, c)
            column = (2 * lax.rem(pz, 2) + lax.div(pz, 4)) * 512
            at = pl.ds(pl.multiple_of(row, 64), 64), pl.ds(pl.multiple_of(column, 512), 512)
            factor[at] = bundles[second][first, high]
    send[...] = nt_dot(factor[:256, :], tok[...])


def project_keep_kernel(factor, tok, keep):
    keep[...] = nt_dot(factor[256:, :], tok[...])


def project(place, bundles, tok, z_first):
    return pl.pallas_call(
        functools.partial(project_kernel, z_first),
        out_shape=(
            jax.ShapeDtypeStruct((256, tok.shape[0]), F32),
            jax.ShapeDtypeStruct((512, 2048), BF16),
        ),
        in_specs=[smem()] + [vmem()] * 5,
        out_specs=(vmem(),) * 2,
        compiler_params=limit(8),
        cost_estimate=estimate(),
        name="project",
    )(place, *bundles, tok)


def score_kernel(p0, p1, p2, p3, resident, out):
    product = total(p0, p1, p2, p3, 0) * total(p0, p1, p2, p3, 1)
    scale = 1.0 / (D * math.sqrt(QTOK))
    here = resident[...].astype(F32)
    for query in range(2):
        summed = jnp.sum(product[QTOK * query : QTOK * query + QTOK], axis=0, keepdims=True)
        out[query : query + 1, :] = summed * scale * here


def score(parts, resident):
    tokens = resident.shape[-1]
    return pl.pallas_call(
        score_kernel,
        out_shape=jax.ShapeDtypeStruct((2, tokens), F32),
        in_specs=[vmem()] * 5,
        out_specs=vmem(),
        compiler_params=limit(6),
        name="score",
    )(*parts, resident)


def local(
    train_acts,
    train_grads,
    query_acts,
    query_grads,
    act_inverse,
    grad_inverse,
    query_slot,
    resident,
):
    dp, width, grid = (lax.axis_index(name) for name in AXES)
    place = jnp.stack([dp // 4, width // 2, dp % 4, width % 2, 4 * grid + dp % 4])
    place, query_slot, query_acts = lax.optimization_barrier((place, query_slot, query_acts))

    def x_others(value):
        out = []
        for step in (2, 1, -1):
            out.append(along_x(value, step))
        return out

    def z_others(value):
        out = [far_z(value)]
        for step in (1, -1):
            out.append(along_z(value, step))
        return out

    def gather(acts, grads):
        ax, gz = x_others(acts), z_others(grads)
        ax, gz = jnp.stack([acts] + ax), jnp.stack([grads] + gz)
        gzx = [gz] + x_others(gz)
        axz = [ax] + z_others(ax)
        return axz, gzx

    bundles = gather(query_acts, query_grads)
    halves = []
    for array, inv in enumerate((act_inverse, grad_inverse)):
        send, rows = precondition(place, query_slot, bundles[array], inv, array == 1)
        got = other_core(send)
        halves.append((kept(rows, inv), got))
    parts = split(*zip(*halves))
    moved = [parts[0]]
    for step in (2, 1, 3):
        moved.append(along_y(parts[step], step))
    factor = factor_sum(moved)
    owner_4 = to_owner(factor, 4)
    owner_0 = to_owner(factor, 0)
    bundles = gather(*(jnp.stack([owner_0[array], owner_4[array]]) for array in range(2)))
    halves = []
    for array, tok in enumerate((train_acts, train_grads)):
        send, rows = project(place, bundles[array], tok, array == 1)
        got = other_core(send)
        halves.append((kept(rows, tok), got))
    parts = split(*zip(*halves))
    moved = [parts[0]]
    for step in (2, 1, 3):
        moved.append(along_y(parts[step], step))
    return score(moved, resident.reshape(1, -1)).T


def solution(mesh):
    return jax.shard_map(
        local,
        mesh=mesh,
        in_specs=(
            P(("dp", "grid"), "width"),
            P(("dp", "grid"), "width"),
            P("dp", "width"),
            P("dp", "width"),
            P(("dp", "grid"), "width"),
            P(("dp", "grid"), "width"),
            P(),
            P(("dp", "grid")),
        ),
        out_specs=P(("dp", "grid"), "width"),
        check_vma=False,
    )
```
